256 devices in a mesh: dp: 32 (over x, z_hi, core), expert: 8 (over y, z_lo).
Axes of the slice: x: 4, y: 4, z: 8 (z_hi: 4, z_lo: 2; z = z_hi * 2 + z_lo), core: 2. Of those that a mesh axis runs over, the one named last changes fastest.
Arguments:
- tokens: bfloat16 [32768, 4096], P(('dp', 'expert')), may hold values from -6 to 6
- cotangent: bfloat16 [32768, 4096], P(('dp', 'expert')), may hold values from -1.1953125 to 1.1953125
- expert_ids: int32 [32768, 2], P(('dp', 'expert')), may hold values from 0 to 63, as said below
- gate_probs: bfloat16 [32768, 2], P(('dp', 'expert')), may hold values from 0.049804688 to 1
- gate_w: bfloat16 [8, 7168, 4096], P('expert', 'dp'), may hold values from -0.09375 to 0.09375
- up_w: bfloat16 [8, 7168, 4096], P('expert', 'dp'), may hold values from -0.09375 to 0.09375
- down_w: bfloat16 [8, 7168, 4096], P('expert', 'dp'), may hold values from -0.0625 to 0.0625
Outputs:
- grad_gate: bfloat16 [8, 7168, 4096], P('expert', 'dp')
- grad_up: bfloat16 [8, 7168, 4096], P('expert', 'dp')
- grad_down: bfloat16 [8, 7168, 4096], P('expert', 'dp')
- grad_probs: float32 [32768, 2], P(('dp', 'expert'))
The draws below stay inside these ranges and needn't reach their ends.
Inputs may be any that keep to these rules, and one draw needn't show every extreme that they name: `expert_ids`: each token names two different experts. Split the rows into aligned blocks of 128 (the rows of one device) and those into aligned runs of 8 blocks: a block names any one expert below 8 at most 4 times, and a run names it at most 16 times; in every draw some block reaches 4 and some run reaches 16.
All inputs are finite; a program needn't handle non-finite values.
Results may differ from the reference program's by a relative error of at most 0.015.
Values may be sent and summed in bfloat16 or wider, within the bound.
No kernel may reach another device: no remote copies, remote signals or barrier semaphores. Data moves between devices by JAX's collectives and lax.ppermute only.
A program may use at most 128 MiB of HBM per device.

```python
import jax
import jax.numpy as jnp

D = 4096
FF = 7168
NE = 64
ROW_CAPACITY = 4
TOK_DEV = 128
EXPERT_COUNT = 8
RECV = 16
TOKENS = 32768
N_DP = 32
DEVICES = 256


def draw_expert_ids(key, part):
    device_groups = DEVICES // EXPERT_COUNT
    random_subkeys = jax.random.split(key, 9)
    busiest_expert = jax.random.randint(random_subkeys[0], (device_groups, 1, 1), 0, EXPERT_COUNT)
    surge_expert = (busiest_expert + 1 + jax.random.randint(random_subkeys[1], (device_groups, 1, 1), 0, EXPERT_COUNT - 1)) % EXPERT_COUNT
    surge_device = jax.random.randint(random_subkeys[2], (device_groups, 1, 1), 0, EXPERT_COUNT)
    ceiling = jax.random.randint(random_subkeys[3], (device_groups, 1, EXPERT_COUNT), 1, ROW_CAPACITY // 2 + 1)
    cold_counts = jax.random.randint(random_subkeys[4], (device_groups, EXPERT_COUNT, EXPERT_COUNT), 0, ceiling + 1)
    expert_dimension = jnp.arange(EXPERT_COUNT)[None, None, :]
    sender_dimension = jnp.arange(EXPERT_COUNT)[None, :, None]
    tally_count = jnp.where(expert_dimension == busiest_expert, ROW_CAPACITY // 2, cold_counts)
    tally_count = jnp.where(expert_dimension == surge_expert, jnp.where(sender_dimension == surge_device, ROW_CAPACITY, 0), tally_count)
    tally_count = tally_count.reshape(DEVICES, EXPERT_COUNT)
    slot_ids = jnp.arange(EXPERT_COUNT * ROW_CAPACITY)
    slot_expert = slot_ids // ROW_CAPACITY
    is_live = (slot_ids % ROW_CAPACITY)[None, :] < tally_count[:, slot_expert]
    chosen = jnp.where(is_live, slot_expert[None, :], -1).astype(jnp.int32)
    orders = jax.vmap(lambda subkey: jax.random.permutation(subkey, TOK_DEV))(jax.random.split(random_subkeys[5], DEVICES))
    window = jnp.full((DEVICES, TOK_DEV), -1, jnp.int32)
    device_rows = jnp.arange(DEVICES)[:, None]
    window = window.at[device_rows, orders[:, :EXPERT_COUNT * ROW_CAPACITY]].set(chosen)
    other_id = jax.random.randint(random_subkeys[6], (DEVICES, TOK_DEV), EXPERT_COUNT, NE)
    offset = jax.random.randint(random_subkeys[7], (DEVICES, TOK_DEV), 1, NE - EXPERT_COUNT)
    second = EXPERT_COUNT + (other_id - EXPERT_COUNT + offset) % (NE - EXPERT_COUNT)
    primary = jnp.where(window >= 0, window, other_id)
    swapped = jax.random.randint(random_subkeys[8], (DEVICES, TOK_DEV), 0, 2)
    left_ids = jnp.where(swapped == 1, second, primary)
    right_ids = jnp.where(swapped == 1, primary, second)
    return jnp.stack([left_ids, right_ids], axis=-1).reshape(TOKENS, 2).astype(jnp.int32)


def levels(key, dims, shards, low, top_value):
    loudness, own = 1.0, jax.random.fold_in(key, 6)
    for position, parts in shards:
        draws = jnp.exp(jax.random.uniform(jax.random.fold_in(own, position), (parts,), jnp.float32, low / len(shards), top_value / len(shards)))
        loudness = loudness * jnp.repeat(draws, dims[position] // parts).reshape([-1 if axis == position else 1 for axis in range(len(dims))])
    return loudness


def gaussian(rng, extent, width, reach, shards=(), dtype=jnp.bfloat16):
    values = width * jax.random.normal(rng, extent, jnp.float32)
    if shards:
        values = values * levels(rng, extent, shards, -0.22, 0.18)
    return jnp.clip(values, -reach, reach).astype(dtype)


def setup_inputs(seed: int = 0) -> dict:
    arg_keys = jax.random.split(jax.random.key(seed), 8)
    tokens = gaussian(arg_keys[0], (TOKENS, D), 1.0, 6.0, ((0, 256),))
    cotangent = gaussian(arg_keys[1], (TOKENS, D), 0.2, 1.1953125, ((0, 256),))
    expert_ids = draw_expert_ids(jax.random.fold_in(arg_keys[7], 71), 0)
    gate_probs = jnp.clip(0.049804688 + 0.9501953 * jax.random.uniform(arg_keys[3], (TOKENS, 2), jnp.float32) ** levels(arg_keys[3], (TOKENS, 2), ((0, 256),), -0.2, 0.2), 0.049804688, 1.0).astype(jnp.bfloat16)
    gate_w = gaussian(arg_keys[4], (EXPERT_COUNT, FF, D), D ** -0.5, 0.09375, ((0, 8), (1, 32)))
    up_w = gaussian(arg_keys[5], (EXPERT_COUNT, FF, D), D ** -0.5, 0.09375, ((0, 8), (1, 32)))
    down_w = gaussian(arg_keys[6], (EXPERT_COUNT, FF, D), FF ** -0.5, 0.0625, ((0, 8), (1, 32)))
    return {"tokens": tokens, "cotangent": cotangent, "expert_ids": expert_ids, "gate_probs": gate_probs, "gate_w": gate_w, "up_w": up_w, "down_w": down_w}


def reference(tokens, cotangent, expert_ids, gate_probs, gate_w, up_w, down_w):
    flat_ids = expert_ids.reshape(-1)
    flat_p = gate_probs.reshape(-1).astype(jnp.float32)
    limit_rows = N_DP * RECV
    grad_flat = jnp.zeros(flat_ids.shape, jnp.float32)
    gates, ups, downs = [], [], []
    for expert in range(EXPERT_COUNT):
        is_hit = flat_ids == expert
        where_hit = jnp.nonzero(is_hit, size=limit_rows, fill_value=0)[0].astype(jnp.int32)
        in_use = jnp.arange(limit_rows) < jnp.sum(is_hit.astype(jnp.int32))
        token_idx = (where_hit // 2).astype(jnp.int32)
        rows_x = tokens[token_idx]
        rows_dy = cotangent[token_idx]
        rows_p = jnp.where(in_use, flat_p[where_hit], 0.0).astype(jnp.float32)
        gate_pre = jnp.dot(rows_x, gate_w[expert].T, preferred_element_type=jnp.float32)
        up_pre = jnp.dot(rows_x, up_w[expert].T, preferred_element_type=jnp.float32)
        sigma = jax.nn.sigmoid(gate_pre)
        hidden = (gate_pre * sigma * up_pre).astype(jnp.bfloat16)
        pulled = jnp.dot(rows_dy, down_w[expert].T, preferred_element_type=jnp.float32)
        router = jnp.sum(hidden.astype(jnp.float32) * pulled, axis=1)
        grad_flat = grad_flat.at[where_hit].add(jnp.where(in_use, router, 0.0))
        scaled_dy = (rows_p[:, None] * rows_dy.astype(jnp.float32)).astype(jnp.bfloat16)
        d_hidden = rows_p[:, None] * pulled
        d_gate = (d_hidden * up_pre * sigma * (1.0 + gate_pre * (1.0 - sigma))).astype(jnp.bfloat16)
        d_up = (d_hidden * gate_pre * sigma).astype(jnp.bfloat16)
        gates.append(jnp.dot(d_gate.T, rows_x, preferred_element_type=jnp.float32).astype(jnp.bfloat16))
        ups.append(jnp.dot(d_up.T, rows_x, preferred_element_type=jnp.float32).astype(jnp.bfloat16))
        downs.append(jnp.dot(hidden.T, scaled_dy, preferred_element_type=jnp.float32).astype(jnp.bfloat16))
    return (jnp.stack(gates), jnp.stack(ups), jnp.stack(downs), grad_flat.reshape(-1, 2))
```

```python
import functools

import jax
import jax.numpy as jnp
from jax import lax
from jax.experimental import pallas as pl
from jax.experimental.pallas import tpu as pltpu
from jax.sharding import Mesh, PartitionSpec as P

CAP = 4
RECV = 16
BF = jnp.bfloat16
F32 = jnp.float32
I32 = jnp.int32
ALL = ("x", "zh", "c", "y", "zl")
SIZES = {"x": 4, "zh": 4, "c": 2, "y": 4, "zl": 2}
VMEM = pl.BlockSpec(memory_space=pltpu.VMEM)


def iota(shape, dim):
    return lax.broadcasted_iota(I32, shape, dim)


def nt(a, b, precision=None):
    return lax.dot_general(
        a, b, (((1,), (1,)), ((), ())), preferred_element_type=F32, precision=precision
    )


def nn(a, b):
    return lax.dot_general(a, b, (((1,), (0,)), ((), ())), preferred_element_type=F32)


def marks(ids):
    n = ids.shape[1]
    rows = iota((8, n), 0)
    first = ids[0:1, :] == rows
    second = ids[1:2, :] == rows
    hit = jnp.where(first | second, 1.0, 0.0).astype(F32)
    earlier = jnp.where(iota((n, n), 0) < iota((n, n), 1), 1.0, 0.0)
    before = nn(hit.astype(BF), earlier.astype(BF))
    return first, second, hit, before


def dispatch_kernel(ids_ref, p_ref, tok_ref, cot_ref, out_ref):
    d = tok_ref.shape[1]
    n = tok_ref.shape[0]
    me = lax.axis_index(ALL).astype(F32)
    first, _, hit, before = marks(ids_ref[...])
    p = p_ref[...].astype(F32)
    weight = jnp.where(first, p[0:1, :], p[1:2, :])
    spread = jnp.where(iota((8 * CAP, 8), 0) // CAP == iota((8 * CAP, 8), 1), 1.0, 0.0)
    spread = spread.astype(BF)
    hit = nn(spread, hit.astype(BF))
    before = nn(spread, before.astype(BF))
    weight = nn(spread, weight.astype(BF))
    rank = (iota((8 * CAP, n), 0) % CAP).astype(F32)
    pick = jnp.where((hit > 0.5) & (before == rank), 1.0, 0.0)
    one = pick.astype(BF)
    x = nn(one, tok_ref[...]).astype(BF)
    dy = nn(one, cot_ref[...]).astype(BF)
    p_col = jnp.sum(pick * weight, axis=1, keepdims=True)
    there = jnp.sum(pick, axis=1, keepdims=True)
    lane = iota((8 * CAP, 128), 1)
    extra = jnp.where(
        lane == 0,
        p_col,
        jnp.where(
            lane == 1, me, jnp.where(lane == 2, rank[:, :128], jnp.where(lane == 3, there, 0.0))
        ),
    ).astype(BF)
    for e in range(8):
        span = slice(e * CAP, (e + 1) * CAP)
        out_ref[e, :, 0:d] = x[span]
        out_ref[e, :, d : 2 * d] = dy[span]
        out_ref[e, :, 2 * d :] = extra[span]


def compact_kernel(in_ref, out_ref, rows_ref):
    w = in_ref.shape[2]
    slots = 8 * CAP
    for e in range(8):
        rows_ref[e * CAP : (e + 1) * CAP, :] = in_ref[e].astype(F32)
    rows = rows_ref[...].astype(BF)
    select = jnp.where(iota((8, 128), 1) == 3, 1.0, 0.0).astype(BF)
    there = nt(select, rows[:, w - 128 :])
    earlier = jnp.where(iota((slots, slots), 0) < iota((slots, slots), 1), 1.0, 0.0).astype(BF)
    place = nn(there.astype(BF), earlier)
    target = iota((RECV, slots), 0).astype(F32)
    pick = jnp.where((there[0:1] > 0.5) & (place[0:1] == target), 1.0, 0.0).astype(BF)
    out_ref[...] = nn(pick, rows).astype(BF)


def forward_kernel(count, last, *refs):
    pieces = refs[:count]
    wg_ref, wu_ref, wd_ref = refs[count : count + 3]
    metas = refs[count + 3 : -4 - last]
    dg_ref, du_ref, hp_ref, meta_ref = refs[len(refs) - 4 - last : len(refs) - last]
    d = wg_ref.shape[1]
    x = jnp.concatenate([r[:, 0:d] for r in pieces], axis=0)
    dy = jnp.concatenate([r[:, d : 2 * d] for r in pieces], axis=0)
    extra = jnp.concatenate([r[:, 2 * d :] for r in pieces], axis=0)
    select = jnp.where(iota((8, 128), 0) == iota((8, 128), 1), 1.0, 0.0).astype(BF)
    info = nt(select, extra)
    p = info[0:1]
    gate = nt(wg_ref[...], x)
    up = nt(wu_ref[...], x)
    pulled = nt(wd_ref[...], dy)
    sigma = 1.0 / (1.0 + jnp.exp(-gate))
    silu = gate * sigma
    hidden = silu * up
    router = jnp.sum(hidden.astype(BF).astype(F32) * pulled, axis=0, keepdims=True)
    d_hidden = p * pulled
    dg_ref[...] = (d_hidden * up * sigma * (1.0 + gate * (1.0 - sigma))).astype(BF)
    du_ref[...] = (d_hidden * silu).astype(BF)
    hp_ref[...] = (p * hidden).astype(BF)
    row = iota(info.shape, 0)
    meta = jnp.where(row == 0, router, info)
    meta_ref[...] = meta
    if last:
        every = jnp.concatenate([m[...] for m in metas] + [meta], axis=1)
        n = every.shape[1]
        owner = iota((256, n), 0).astype(F32)
        spread = jnp.where(every[1:2] == owner, every[0:1], 0.0)
        lanes = iota((128, n), 0).astype(F32)
        rank = jnp.where(every[2:3] == lanes, 1.0, 0.0)
        refs[-1][...] = nt(spread, rank, lax.Precision.HIGHEST)


def backward_kernel(count, groups, *refs):
    pieces_x = refs[:count]
    pieces_dy = refs[count : 2 * count]
    at = 2 * count
    dg = jnp.concatenate([r[...] for r in refs[at : at + groups]], axis=1)
    du = jnp.concatenate([r[...] for r in refs[at + groups : at + 2 * groups]], axis=1)
    hp = jnp.concatenate([r[...] for r in refs[at + 2 * groups : at + 3 * groups]], axis=1)
    og_ref, ou_ref, od_ref = refs[at + 3 * groups :]
    x = jnp.concatenate([r[...] for r in pieces_x], axis=0)
    dy = jnp.concatenate([r[...] for r in pieces_dy], axis=0)
    og_ref[0] = nn(dg, x).astype(BF)
    ou_ref[0] = nn(du, x).astype(BF)
    od_ref[0] = nn(hp, dy).astype(BF)


def collect_kernel(got_ref, ids_ref, out_ref):
    first, second, _, before = marks(ids_ref[...])
    total = got_ref[0:8, :]
    for i in range(1, got_ref.shape[0] // 8):
        total = total + got_ref[8 * i : 8 * i + 8, :]
    value = jnp.zeros(before.shape, F32)
    for j in range(CAP):
        value = value + jnp.where(before == j, total[:, j : j + 1], 0.0)
    out_ref[0:1, :] = jnp.sum(jnp.where(first, value, 0.0), axis=0, keepdims=True)
    out_ref[1:2, :] = jnp.sum(jnp.where(second, value, 0.0), axis=0, keepdims=True)


PARAMS = pltpu.CompilerParams(vmem_limit_bytes=48 * 1024 * 1024)


def move(a, axis, shift):
    n = SIZES[axis]
    return lax.ppermute(a, axis, [(i, (i + shift) % n) for i in range(n)])


def ring(s, axis):
    half = s.shape[0] // 2
    right = move(s, axis, 1)
    left = move(s, axis, 3)
    far_a = move(right[:half], axis, 1)
    far_b = move(left[half:], axis, 3)
    return jnp.concatenate([s, right, left, far_a, far_b], axis=0)


def shards(tokens, cotangent, expert_ids, gate_probs, gate_w, up_w, down_w):
    n, d = tokens.shape
    hid = gate_w.shape[1]
    w = 2 * d + 128
    ids = expert_ids.T
    send = pl.pallas_call(
        dispatch_kernel,
        out_shape=jax.ShapeDtypeStruct((8, CAP, w), BF),
        in_specs=[VMEM] * 4,
        out_specs=VMEM,
        compiler_params=PARAMS,
        name="dispatch",
    )(ids, gate_probs.T, tokens, cotangent)
    got = lax.all_to_all(send, ("y", "zl"), split_axis=0, concat_axis=0, tiled=True)
    s = pl.pallas_call(
        compact_kernel,
        out_shape=jax.ShapeDtypeStruct((RECV, w), BF),
        in_specs=[VMEM],
        out_specs=VMEM,
        scratch_shapes=[pltpu.VMEM((8 * CAP, w), F32)],
        compiler_params=PARAMS,
        name="compact",
    )(got)

    half = RECV // 2
    right = move(s, "zh", 1)
    left = move(s, "zh", 3)
    group0 = ring(s, "x")
    far = jnp.concatenate([move(right[:half], "zh", 1), move(left[half:], "zh", 3)], axis=0)
    group1 = ring(jnp.concatenate([right, left], axis=0), "x")
    group2 = ring(far, "x")
    groups = [(g, move(g, "c", 1)) for g in (group0, group1, group2)]

    weights = (gate_w[0], up_w[0], down_w[0])
    metas, dgs, dus, hps = [], [], [], []
    for i, pieces in enumerate(groups):
        last = i == len(groups) - 1
        rows = sum(q.shape[0] for q in pieces)
        outs = [jax.ShapeDtypeStruct((hid, rows), BF)] * 3
        outs.append(jax.ShapeDtypeStruct((8, rows), F32))
        if last:
            outs.append(jax.ShapeDtypeStruct((256, 128), F32))
        before = tuple(metas) if last else ()
        res = pl.pallas_call(
            functools.partial(forward_kernel, len(pieces), int(last)),
            out_shape=outs,
            in_specs=[VMEM] * (len(pieces) + 3 + len(before)),
            out_specs=[VMEM] * len(outs),
            compiler_params=PARAMS,
            name="forward",
        )(*pieces, *weights, *before)
        dgs.append(res[0])
        dus.append(res[1])
        hps.append(res[2])
        metas.append(res[3])
    router = res[4]
    returned = lax.all_to_all(router, ALL, split_axis=0, concat_axis=0, tiled=True)

    flat = [q for pieces in groups for q in pieces]
    blk = 512
    steps = d // blk
    specs = [pl.BlockSpec((q.shape[0], blk), lambda j: (0, j)) for q in flat]
    specs += [
        pl.BlockSpec((q.shape[0], blk), lambda j, off=steps: (0, j + off)) for q in flat
    ]
    for q in dgs + dus + hps:
        specs.append(pl.BlockSpec(q.shape, lambda j: (0, 0)))
    grads = pl.pallas_call(
        functools.partial(backward_kernel, len(flat), len(dgs)),
        out_shape=[jax.ShapeDtypeStruct((1, hid, d), BF)] * 3,
        grid=(steps,),
        in_specs=specs,
        out_specs=[pl.BlockSpec((1, hid, blk), lambda j: (0, 0, j))] * 3,
        compiler_params=PARAMS,
        name="backward",
    )(*flat, *flat, *dgs, *dus, *hps)

    grad_probs = pl.pallas_call(
        collect_kernel,
        out_shape=jax.ShapeDtypeStruct((2, n), F32),
        in_specs=[VMEM] * 2,
        out_specs=VMEM,
        compiler_params=PARAMS,
        name="collect",
    )(returned, ids)
    return (*grads, grad_probs.T)


def solution(mesh):
    fine = Mesh(mesh.devices.reshape([SIZES[a] for a in ALL]), ALL)
    dp, ex = ("x", "zh", "c"), ("y", "zl")
    rows = P(ALL, None)
    kept = P(ex, dp, None)
    return jax.shard_map(
        shards,
        mesh=fine,
        in_specs=(rows,) * 4 + (kept,) * 3,
        out_specs=(kept,) * 3 + (rows,),
        check_vma=False,
    )
```

```python
import functools

import jax
import jax.numpy as jnp
from jax import lax
from jax.experimental import pallas as pl
from jax.experimental.pallas import tpu as pltpu
from jax.sharding import Mesh, PartitionSpec as P

CAP = 4
RECV = 16
BF = jnp.bfloat16
F32 = jnp.float32
I32 = jnp.int32
ALL = ("x", "zh", "c", "y", "zl")
SIZES = {"x": 4, "zh": 4, "c": 2, "y": 4, "zl": 2}
VMEM = pl.BlockSpec(memory_space=pltpu.VMEM)
HBM = pl.BlockSpec(memory_space=pltpu.HBM)


def iota(shape, dim):
    return lax.broadcasted_iota(I32, shape, dim)


def nt(a, b, precision=None):
    return lax.dot_general(
        a, b, (((1,), (1,)), ((), ())), preferred_element_type=F32, precision=precision
    )


def nn(a, b):
    return lax.dot_general(a, b, (((1,), (0,)), ((), ())), preferred_element_type=F32)


def marks(ids):
    n = ids.shape[1]
    rows = iota((8, n), 0)
    first = ids[0:1, :] == rows
    second = ids[1:2, :] == rows
    hit = jnp.where(first | second, 1.0, 0.0).astype(F32)
    earlier = jnp.where(iota((n, n), 0) < iota((n, n), 1), 1.0, 0.0)
    before = nn(hit.astype(BF), earlier.astype(BF))
    return first, second, hit, before


def dispatch_kernel(
    ids_hbm, p_hbm, tok_hbm, cot_hbm, out_ref, ids_ref, p_ref, tok_ref, cot_ref, sems
):
    copies = [
        pltpu.make_async_copy(a, b, sems.at[i])
        for i, (a, b) in enumerate(
            ((ids_hbm, ids_ref), (p_hbm, p_ref), (tok_hbm, tok_ref), (cot_hbm, cot_ref))
        )
    ]
    for c in copies:
        c.start()
    d = tok_ref.shape[1]
    n = tok_ref.shape[0]
    copies[0].wait()
    copies[1].wait()
    me = lax.axis_index(ALL).astype(F32)
    first, _, hit, before = marks(ids_ref[...])
    p = p_ref[...].astype(F32)
    weight = jnp.where(first, p[0:1, :], p[1:2, :])
    spread = jnp.where(iota((8 * CAP, 8), 0) // CAP == iota((8 * CAP, 8), 1), 1.0, 0.0)
    spread = spread.astype(BF)
    hit = nn(spread, hit.astype(BF))
    before = nn(spread, before.astype(BF))
    weight = nn(spread, weight.astype(BF))
    rank = (iota((8 * CAP, n), 0) % CAP).astype(F32)
    pick = jnp.where((hit > 0.5) & (before == rank), 1.0, 0.0)
    one = pick.astype(BF)
    copies[2].wait()
    x = nn(one, tok_ref[...]).astype(BF)
    copies[3].wait()
    dy = nn(one, cot_ref[...]).astype(BF)
    p_col = jnp.sum(pick * weight, axis=1, keepdims=True)
    there = jnp.sum(pick, axis=1, keepdims=True)
    lane = iota((8 * CAP, 128), 1)
    extra = jnp.where(
        lane == 0,
        p_col,
        jnp.where(
            lane == 1, me, jnp.where(lane == 2, rank[:, :128], jnp.where(lane == 3, there, 0.0))
        ),
    ).astype(BF)
    for e in range(8):
        span = slice(e * CAP, (e + 1) * CAP)
        out_ref[e, :, 0:d] = x[span]
        out_ref[e, :, d : 2 * d] = dy[span]
        out_ref[e, :, 2 * d :] = extra[span]


def compact_kernel(in_ref, out_ref, rows_ref):
    w = in_ref.shape[2]
    slots = 8 * CAP
    for e in range(8):
        rows_ref[e * CAP : (e + 1) * CAP, :] = in_ref[e].astype(F32)
    rows = rows_ref[...].astype(BF)
    select = jnp.where(iota((8, 128), 1) == 3, 1.0, 0.0).astype(BF)
    there = nt(select, rows[:, w - 128 :])
    earlier = jnp.where(iota((slots, slots), 0) < iota((slots, slots), 1), 1.0, 0.0).astype(BF)
    place = nn(there.astype(BF), earlier)
    target = iota((RECV, slots), 0).astype(F32)
    pick = jnp.where((there[0:1] > 0.5) & (place[0:1] == target), 1.0, 0.0).astype(BF)
    out_ref[...] = nn(pick, rows).astype(BF)


def forward_kernel(spans, last, *refs):
    count = len(spans)
    *refs, dg_buf, du_buf, hp_buf, sems = refs
    pieces = [r.at[lo:hi] for r, (lo, hi) in zip(refs[:count], spans)]
    wg_ref, wu_ref, wd_ref = refs[count : count + 3]
    metas = refs[count + 3 : -5 - last]
    rows_ref, dg_ref, du_ref, hp_ref, meta_ref = refs[len(refs) - 5 - last : len(refs) - last]
    d = wg_ref.shape[1]
    copies = []
    at = 0
    for i, (lo, hi) in enumerate(spans):
        copies.append(
            pltpu.make_async_copy(pieces[i], rows_ref.at[at : at + hi - lo], sems.at[3 + i])
        )
        copies[-1].start()
        at += hi - lo
    x = jnp.concatenate([r[:, 0:d] for r in pieces], axis=0)
    dy = jnp.concatenate([r[:, d : 2 * d] for r in pieces], axis=0)
    extra = jnp.concatenate([r[:, 2 * d :] for r in pieces], axis=0)
    select = jnp.where(iota((8, 128), 0) == iota((8, 128), 1), 1.0, 0.0).astype(BF)
    info = nt(select, extra)
    p = info[0:1]
    gate = nt(wg_ref[...], x)
    up = nt(wu_ref[...], x)
    pulled = nt(wd_ref[...], dy)
    sigma = 1.0 / (1.0 + jnp.exp(-gate))
    silu = gate * sigma
    hidden = silu * up
    router = jnp.sum(hidden.astype(BF).astype(F32) * pulled, axis=0, keepdims=True)
    d_hidden = p * pulled
    dg_buf[...] = (d_hidden * up * sigma * (1.0 + gate * (1.0 - sigma))).astype(BF)
    du_buf[...] = (d_hidden * silu).astype(BF)
    hp_buf[...] = (p * hidden).astype(BF)
    for i, (a, b) in enumerate(((dg_buf, dg_ref), (du_buf, du_ref), (hp_buf, hp_ref))):
        copies.append(pltpu.make_async_copy(a, b, sems.at[i]))
        copies[-1].start()
    row = iota(info.shape, 0)
    meta = jnp.where(row == 0, router, info)
    meta_ref[...] = meta
    if last:
        every = jnp.concatenate([m[...] for m in metas] + [meta], axis=1)
        n = every.shape[1]
        owner = iota((256, n), 0).astype(F32)
        own = jnp.where(every[1:2] == owner, 1.0, 0.0).astype(BF)
        rest = every[0:1]
        parts = []
        for _ in range(3):
            top = rest.astype(BF)
            parts.append(top.astype(F32))
            rest = rest - parts[-1]
        place = iota((32, n), 0)
        value = jnp.where(place < 8, parts[0], jnp.where(place < 16, parts[1], parts[2]))
        rank = (place % 8).astype(F32)
        live = (every[2:3] == rank) & (place < 24)
        value = jnp.where(live, value, 0.0).astype(BF)
        value = jnp.concatenate([value, jnp.zeros((96, n), BF)], axis=0)
        refs[-1][...] = nt(own, value)
    for c in copies:
        c.wait()


def backward_kernel(count, groups, *refs):
    pieces = refs[:count]
    factors = refs[count : count + 3 * groups]
    outs = refs[count + 3 * groups : count + 3 * groups + 3]
    rows_ref, *fact = refs[count + 3 * groups + 3 : count + 3 * groups + 5 + groups - 1]
    bufs = refs[-6:-3]
    rows_sem, fact_sem, out_sem = refs[-3:]
    d = outs[0].shape[2]
    blk = bufs[0].shape[2]
    steps = d // blk
    loads = []
    for g in range(groups):
        for k in range(3):
            c = pltpu.make_async_copy(
                factors[k * groups + g], fact[g].at[k], fact_sem.at[g, k]
            )
            c.start()
            loads.append(c)
    fetch = []
    for j in range(steps):
        some = []
        for k in range(2):
            cols = slice(k * d + j * blk, k * d + (j + 1) * blk)
            at = 0
            for i, r in enumerate(pieces):
                c = pltpu.make_async_copy(
                    r.at[:, cols],
                    rows_ref.at[at : at + r.shape[0], cols],
                    rows_sem.at[j, k * count + i],
                )
                c.start()
                some.append(c)
                at += r.shape[0]
        fetch.append(some)
    for c in loads:
        c.wait()
    hid = fact[0].shape[1]
    both = jnp.concatenate(
        [jnp.concatenate([f[k] for f in fact], axis=1) for k in range(2)], axis=0
    )
    hp = jnp.concatenate([f[2] for f in fact], axis=1)
    flying = {}
    for j in range(steps):
        slot = j % 2
        here = slice(j * blk, (j + 1) * blk)
        there = slice(d + j * blk, d + (j + 1) * blk)
        for c in fetch[j]:
            c.wait()
        two = nn(both, rows_ref[:, here]).astype(BF)
        one = nn(hp, rows_ref[:, there]).astype(BF)
        for k, value in enumerate((two[:hid], two[hid:], one)):
            if j >= 2:
                flying[k, slot].wait()
            bufs[k][slot] = value
            flying[k, slot] = pltpu.make_async_copy(
                bufs[k].at[slot], outs[k].at[0, :, here], out_sem.at[k, slot]
            )
            flying[k, slot].start()
    for c in flying.values():
        c.wait()


def collect_kernel(got_ref, ids_ref, out_ref):
    first, second, _, before = marks(ids_ref[...])
    total = got_ref[0:8, :]
    for i in range(1, got_ref.shape[0] // 8):
        total = total + got_ref[8 * i : 8 * i + 8, :]
    value = jnp.zeros(before.shape, F32)
    for j in range(CAP):
        sums = total[:, j : j + 1] + total[:, 8 + j : 9 + j] + total[:, 16 + j : 17 + j]
        value = value + jnp.where(before == j, sums, 0.0)
    out_ref[0:1, :] = jnp.sum(jnp.where(first, value, 0.0), axis=0, keepdims=True)
    out_ref[1:2, :] = jnp.sum(jnp.where(second, value, 0.0), axis=0, keepdims=True)


def in_hbm(*arrays):
    return [pltpu.with_memory_space_constraint(a, pltpu.HBM) for a in arrays]


def limit(mib):
    return pltpu.CompilerParams(vmem_limit_bytes=mib * 1024 * 1024)


def move(a, axis, shift):
    n = SIZES[axis]
    return lax.ppermute(a, axis, [(i, (i + shift) % n) for i in range(n)])


def gate(a, *after):
    return lax.optimization_barrier((a,) + after)[0]


def shards(tokens, cotangent, expert_ids, gate_probs, gate_w, up_w, down_w):
    n, d = tokens.shape
    hid = gate_w.shape[1]
    w = 2 * d + 128
    ids = expert_ids.T
    send = pl.pallas_call(
        dispatch_kernel,
        out_shape=jax.ShapeDtypeStruct((8, CAP, w), BF),
        in_specs=[HBM] * 4,
        out_specs=VMEM,
        scratch_shapes=[
            pltpu.VMEM((2, n), I32),
            pltpu.VMEM((2, n), BF),
            pltpu.VMEM((n, d), BF),
            pltpu.VMEM((n, d), BF),
            pltpu.SemaphoreType.DMA((4,)),
        ],
        compiler_params=limit(8),
        name="dispatch",
    )(*in_hbm(ids, gate_probs.T, tokens, cotangent))
    got = lax.all_to_all(send, ("y", "zl"), split_axis=0, concat_axis=0, tiled=True)
    s = pl.pallas_call(
        compact_kernel,
        out_shape=jax.ShapeDtypeStruct((RECV, w), BF),
        in_specs=[VMEM],
        out_specs=VMEM,
        scratch_shapes=[pltpu.VMEM((8 * CAP, w), F32)],
        compiler_params=limit(4),
        name="compact",
    )(got)

    half = RECV
    z_r = move(s, "zh", 1)
    z_l = move(s, "zh", 3)
    x_r = move(s, "x", 1)
    x_l = move(s, "x", 3)
    x_2 = move(s, "x", 2)
    row_a = jnp.concatenate([s, x_r, x_l, x_2], axis=0)
    near = gate(jnp.concatenate([z_r, z_l], axis=0), x_r, x_l, x_2)
    near_r = move(near, "x", 1)
    near_l = move(near, "x", 3)
    far = move(gate(s, z_r, z_l), "zh", 2)
    row_b = jnp.concatenate([near, near_r, near_l, far], axis=0)
    far_r = move(jnp.concatenate([near_r[:half], far], axis=0), "x", 1)
    far_l = move(jnp.concatenate([near_l[half:], far], axis=0), "x", 3)
    far_x = move(gate(x_2, far), "zh", 2)
    row_c = jnp.concatenate([far_r, far_l, far_x], axis=0)
    other_a = move(row_a, "c", 1)
    other_b = move(row_b, "c", 1)
    other_c = move(gate(row_c, other_a, other_b), "c", 1)
    flat = [row_a, other_a, row_b, other_b, row_c, other_c]

    weights = (gate_w[0], up_w[0], down_w[0])
    size = sum(q.shape[0] for q in flat) // 2
    calls = ([], [])
    at = 0
    for q in flat:
        n_q = q.shape[0]
        cut = min(max(size - at, 0), n_q)
        if cut:
            calls[0].append((q, 0, cut))
        if cut < n_q:
            calls[1].append((q, cut, n_q))
        at += n_q
    stored, metas, factors = [], [], []
    for i, pieces in enumerate(calls):
        last = i == len(calls) - 1
        outs = [pltpu.HBM((size, w), BF)] + [pltpu.HBM((hid, size), BF)] * 3
        outs.append(jax.ShapeDtypeStruct((8, size), F32))
        if last:
            outs.append(jax.ShapeDtypeStruct((256, 128), F32))
        before = tuple(metas) if last else ()
        res = pl.pallas_call(
            functools.partial(forward_kernel, [q[1:] for q in pieces], int(last)),
            out_shape=outs,
            in_specs=[VMEM] * (len(pieces) + 3 + len(before)),
            out_specs=[HBM] * 4 + [VMEM] * (len(outs) - 4),
            scratch_shapes=[pltpu.VMEM((hid, size), BF)] * 3
            + [pltpu.SemaphoreType.DMA((3 + len(pieces),))],
            compiler_params=limit(16),
            name="forward",
        )(*[q[0] for q in pieces], *weights, *before)
        stored.append(res[0])
        factors.append(res[1:4])
        metas.append(res[4])
    router = res[5]
    returned = lax.all_to_all(router, ALL, split_axis=0, concat_axis=0, tiled=True)

    blk = 512
    count = len(stored)
    grads = pl.pallas_call(
        functools.partial(backward_kernel, count, count),
        out_shape=[jax.ShapeDtypeStruct((1, hid, d), BF)] * 3,
        in_specs=[HBM] * (4 * count),
        out_specs=[HBM] * 3,
        scratch_shapes=[pltpu.VMEM((count * size, w), BF)]
        + [pltpu.VMEM((3, hid, size), BF)] * count
        + [pltpu.VMEM((2, hid, blk), BF)] * 3
        + [
            pltpu.SemaphoreType.DMA((d // blk, 2 * count)),
            pltpu.SemaphoreType.DMA((count, 3)),
            pltpu.SemaphoreType.DMA((3, 2)),
        ],
        compiler_params=limit(24),
        name="backward",
    )(*in_hbm(*stored, *[f[k] for k in range(3) for f in factors]))

    grad_probs = pl.pallas_call(
        collect_kernel,
        out_shape=jax.ShapeDtypeStruct((2, n), F32),
        in_specs=[VMEM] * 2,
        out_specs=VMEM,
        compiler_params=limit(4),
        name="collect",
    )(returned, ids)
    return (*grads, grad_probs.T)


def solution(mesh):
    fine = Mesh(mesh.devices.reshape([SIZES[a] for a in ALL]), ALL)
    dp, ex = ("x", "zh", "c"), ("y", "zl")
    rows = P(ALL, None)
    kept = P(ex, dp, None)
    return jax.shard_map(
        shards,
        mesh=fine,
        in_specs=(rows,) * 4 + (kept,) * 3,
        out_specs=(kept,) * 3 + (rows,),
        check_vma=False,
    )
```

```python
import functools

import jax
import jax.numpy as jnp
from jax import lax
from jax.experimental import pallas as pl
from jax.experimental.pallas import tpu as pltpu
from jax.sharding import Mesh, PartitionSpec as P

CAP = 4
RECV = 16
BF = jnp.bfloat16
F32 = jnp.float32
I32 = jnp.int32
ALL = ("x", "zh", "c", "y", "zl")
SIZES = {"x": 4, "zh": 4, "c": 2, "y": 4, "zl": 2}
VMEM = pl.BlockSpec(memory_space=pltpu.VMEM)
HBM = pl.BlockSpec(memory_space=pltpu.HBM)


def iota(shape, dim):
    return lax.broadcasted_iota(I32, shape, dim)


def nt(a, b, precision=None):
    return lax.dot_general(
        a, b, (((1,), (1,)), ((), ())), preferred_element_type=F32, precision=precision
    )


def nn(a, b):
    return lax.dot_general(a, b, (((1,), (0,)), ((), ())), preferred_element_type=F32)


def marks(ids):
    n = ids.shape[1]
    rows = iota((8, n), 0)
    first = ids[0:1, :] == rows
    second = ids[1:2, :] == rows
    hit = jnp.where(first | second, 1.0, 0.0).astype(F32)
    earlier = jnp.where(iota((n, n), 0) < iota((n, n), 1), 1.0, 0.0)
    before = nn(hit.astype(BF), earlier.astype(BF))
    return first, second, hit, before


def dispatch_kernel(
    ids_hbm, p_hbm, tok_hbm, cot_hbm, out_ref, ids_ref, p_ref, tok_ref, cot_ref, sems
):
    copies = [
        pltpu.make_async_copy(a, b, sems.at[i])
        for i, (a, b) in enumerate(
            ((ids_hbm, ids_ref), (p_hbm, p_ref), (tok_hbm, tok_ref), (cot_hbm, cot_ref))
        )
    ]
    for c in copies:
        c.start()
    d = tok_ref.shape[1]
    n = tok_ref.shape[0]
    copies[0].wait()
    copies[1].wait()
    me = lax.axis_index(ALL).astype(F32)
    first, _, hit, before = marks(ids_ref[...])
    p = p_ref[...].astype(F32)
    weight = jnp.where(first, p[0:1, :], p[1:2, :])
    spread = jnp.where(iota((8 * CAP, 8), 0) // CAP == iota((8 * CAP, 8), 1), 1.0, 0.0)
    spread = spread.astype(BF)
    hit = nn(spread, hit.astype(BF))
    before = nn(spread, before.astype(BF))
    weight = nn(spread, weight.astype(BF))
    rank = (iota((8 * CAP, n), 0) % CAP).astype(F32)
    pick = jnp.where((hit > 0.5) & (before == rank), 1.0, 0.0)
    one = pick.astype(BF)
    copies[2].wait()
    x = nn(one, tok_ref[...]).astype(BF)
    copies[3].wait()
    dy = nn(one, cot_ref[...]).astype(BF)
    p_col = jnp.sum(pick * weight, axis=1, keepdims=True)
    there = jnp.sum(pick, axis=1, keepdims=True)
    lane = iota((8 * CAP, 128), 1)
    extra = jnp.where(
        lane == 0,
        p_col,
        jnp.where(
            lane == 1, me, jnp.where(lane == 2, rank[:, :128], jnp.where(lane == 3, there, 0.0))
        ),
    ).astype(BF)
    for e in range(8):
        span = slice(e * CAP, (e + 1) * CAP)
        out_ref[e, :, 0:d] = x[span]
        out_ref[e, :, d : 2 * d] = dy[span]
        out_ref[e, :, 2 * d :] = extra[span]


def compact_kernel(in_ref, out_ref, rows_ref):
    w = in_ref.shape[2]
    slots = 8 * CAP
    for e in range(8):
        rows_ref[e * CAP : (e + 1) * CAP, :] = in_ref[e].astype(F32)
    rows = rows_ref[...].astype(BF)
    select = jnp.where(iota((8, 128), 1) == 3, 1.0, 0.0).astype(BF)
    there = nt(select, rows[:, w - 128 :])
    earlier = jnp.where(iota((slots, slots), 0) < iota((slots, slots), 1), 1.0, 0.0).astype(BF)
    place = nn(there.astype(BF), earlier)
    target = iota((RECV, slots), 0).astype(F32)
    pick = jnp.where((there[0:1] > 0.5) & (place[0:1] == target), 1.0, 0.0).astype(BF)
    out_ref[...] = nn(pick, rows).astype(BF)


def forward(pieces, wg_ref, wu_ref, wd_ref):
    d = wg_ref.shape[1]
    x = jnp.concatenate([r[:, 0:d] for r in pieces], axis=0)
    dy = jnp.concatenate([r[:, d : 2 * d] for r in pieces], axis=0)
    extra = jnp.concatenate([r[:, 2 * d :] for r in pieces], axis=0)
    select = jnp.where(iota((8, 128), 0) == iota((8, 128), 1), 1.0, 0.0).astype(BF)
    info = nt(select, extra)
    p = info[0:1]
    gate = nt(wg_ref[...], x)
    up = nt(wu_ref[...], x)
    pulled = nt(wd_ref[...], dy)
    sigma = 1.0 / (1.0 + jnp.exp(-gate))
    silu = gate * sigma
    hidden = silu * up
    router = jnp.sum(hidden.astype(BF).astype(F32) * pulled, axis=0, keepdims=True)
    d_hidden = p * pulled
    dg = (d_hidden * up * sigma * (1.0 + gate * (1.0 - sigma))).astype(BF)
    du = (d_hidden * silu).astype(BF)
    hp = (p * hidden).astype(BF)
    return dg, du, hp, jnp.where(iota(info.shape, 0) == 0, router, info)


def first_kernel(spans, *refs):
    count = len(spans)
    pieces = [r.at[lo:hi] for r, (lo, hi) in zip(refs[:count], spans)]
    wg_ref, wu_ref, wd_ref, meta_ref, part_ref, rows_ref, buf, sems, rows_sem = refs[count:]
    hid, d = wg_ref.shape
    left = pltpu.make_async_copy(
        refs[count - 1].at[spans[-1][1] : refs[count - 1].shape[0]], rows_ref, rows_sem.at[0]
    )
    left.start()
    dg, du, hp, meta_ref[...] = forward(pieces, wg_ref, wu_ref, wd_ref)
    both = jnp.concatenate([dg, du], axis=0)
    blk = buf.shape[3]
    flying = {}
    for j in range(d // blk):
        slot = j % 2
        here = slice(j * blk, (j + 1) * blk)
        there = slice(d + j * blk, d + (j + 1) * blk)
        two = nn(both, jnp.concatenate([r[:, here] for r in pieces], axis=0))
        one = nn(hp, jnp.concatenate([r[:, there] for r in pieces], axis=0))
        for k, value in enumerate((two[:hid], two[hid:], one)):
            if j >= 2:
                flying[k, slot].wait()
            buf[slot, k] = value.astype(BF)
            flying[k, slot] = pltpu.make_async_copy(
                buf.at[slot, k], part_ref.at[k, :, here], sems.at[slot, k]
            )
            flying[k, slot].start()
    left.wait()
    for c in flying.values():
        c.wait()


def last_kernel(spans, *refs):
    count = len(spans)
    pieces = [r.at[lo:hi] for r, (lo, hi) in zip(refs[:count], spans)]
    (
        wg_ref, wu_ref, wd_ref, other_ref, rows_ref, fact_ref, router_ref, fact_buf, sems
    ) = refs[count:]
    copies = []
    at = 0
    for i, (lo, hi) in enumerate(spans):
        if i == 0:
            continue
        n = hi - lo
        copies.append(
            pltpu.make_async_copy(pieces[i], rows_ref.at[at : at + n], sems.at[i])
        )
        copies[-1].start()
        at += n
    *three, meta = forward(pieces, wg_ref, wu_ref, wd_ref)
    for k, value in enumerate(three):
        fact_buf[k] = value
        copies.append(
            pltpu.make_async_copy(fact_buf.at[k], fact_ref.at[k], sems.at[count + k])
        )
        copies[-1].start()
    every = jnp.concatenate([other_ref[...], meta], axis=1)
    n = every.shape[1]
    group = jnp.floor(every[1:2] * 0.125)
    slot = (every[1:2] - 8.0 * group) * CAP + every[2:3]
    own = jnp.where(group == iota((32, n), 0).astype(F32), 1.0, 0.0).astype(BF)
    rest = every[0:1]
    parts = []
    for _ in range(3):
        top = rest.astype(BF)
        parts.append(top.astype(F32))
        rest = rest - parts[-1]
    place = iota((128, n), 0)
    value = jnp.where(place < 32, parts[0], jnp.where(place < 64, parts[1], parts[2]))
    live = ((place % 32).astype(F32) == slot) & (place < 96)
    value = jnp.where(live, value, 0.0).astype(BF)
    moved = nt(own, value)
    mine = (iota((8, 128), 1) % 32) // CAP == iota((8, 128), 0)
    for i in range(32):
        router_ref[8 * i : 8 * i + 8, :] = jnp.where(mine, moved[i : i + 1, :], 0.0)
    for c in copies:
        c.wait()


def backward_kernel(left_hbm, rows_hbm, fact_hbm, part_hbm, *refs):
    outs = refs[:3]
    rows_ref, fact_ref, part_ref, buf, fact_sem, rows_sem, part_sem, out_sem = refs[3:]
    hid, d = part_ref.shape[1:]
    blk = buf.shape[3]
    steps = d // blk
    fact = pltpu.make_async_copy(fact_hbm, fact_ref, fact_sem.at[0])
    fact.start()
    fetch = []
    for j in range(steps):
        some = []
        for k in range(2):
            cols = slice(k * d + j * blk, k * d + (j + 1) * blk)
            cut = left_hbm.shape[0]
            some.append(
                pltpu.make_async_copy(
                    left_hbm.at[:, cols], rows_ref.at[0:cut, cols], rows_sem.at[j, 2 * k]
                )
            )
            some.append(
                pltpu.make_async_copy(
                    rows_hbm.at[:, cols], rows_ref.at[cut:, cols], rows_sem.at[j, 2 * k + 1]
                )
            )
        cols = slice(j * blk, (j + 1) * blk)
        some.append(
            pltpu.make_async_copy(part_hbm.at[:, :, cols], part_ref.at[:, :, cols], part_sem.at[j])
        )
        for c in some:
            c.start()
        fetch.append(some)
    fact.wait()
    both = jnp.concatenate([fact_ref[0], fact_ref[1]], axis=0)
    hp = fact_ref[2]
    flying = {}
    for j in range(steps):
        slot = j % 2
        here = slice(j * blk, (j + 1) * blk)
        there = slice(d + j * blk, d + (j + 1) * blk)
        for c in fetch[j]:
            c.wait()
        two = nn(both, rows_ref[:, here])
        one = nn(hp, rows_ref[:, there])
        for k, value in enumerate((two[:hid], two[hid:], one)):
            if j >= 2:
                flying[k, slot].wait()
            buf[slot, k] = (value + part_ref[k, :, here].astype(F32)).astype(BF)
            flying[k, slot] = pltpu.make_async_copy(
                buf.at[slot, k], outs[k].at[0, :, here], out_sem.at[slot, k]
            )
            flying[k, slot].start()
    for c in flying.values():
        c.wait()


def collect_kernel(got_ref, ids_ref, out_ref):
    first, second, _, before = marks(ids_ref[...])
    total = got_ref[0:8, :]
    for i in range(1, got_ref.shape[0] // 8):
        total = total + got_ref[8 * i : 8 * i + 8, :]
    value = jnp.zeros(before.shape, F32)
    for j in range(CAP):
        mine = iota(total.shape, 1) % CAP == j
        sums = jnp.sum(jnp.where(mine, total, 0.0), axis=1, keepdims=True)
        value = value + jnp.where(before == j, sums, 0.0)
    out_ref[0:1, :] = jnp.sum(jnp.where(first, value, 0.0), axis=0, keepdims=True)
    out_ref[1:2, :] = jnp.sum(jnp.where(second, value, 0.0), axis=0, keepdims=True)


def in_hbm(*arrays):
    return [pltpu.with_memory_space_constraint(a, pltpu.HBM) for a in arrays]


def limit(mib):
    return pltpu.CompilerParams(vmem_limit_bytes=mib * 1024 * 1024)


def move(a, axis, shift):
    n = SIZES[axis]
    return lax.ppermute(a, axis, [(i, (i + shift) % n) for i in range(n)])


def gate(a, *after):
    return lax.optimization_barrier((a,) + after)[0]


def shards(tokens, cotangent, expert_ids, gate_probs, gate_w, up_w, down_w):
    n, d = tokens.shape
    hid = gate_w.shape[1]
    w = 2 * d + 128
    ids = expert_ids.T
    send = pl.pallas_call(
        dispatch_kernel,
        out_shape=jax.ShapeDtypeStruct((8, CAP, w), BF),
        in_specs=[HBM] * 4,
        out_specs=VMEM,
        scratch_shapes=[
            pltpu.VMEM((2, n), I32),
            pltpu.VMEM((2, n), BF),
            pltpu.VMEM((n, d), BF),
            pltpu.VMEM((n, d), BF),
            pltpu.SemaphoreType.DMA((4,)),
        ],
        compiler_params=limit(8),
        name="dispatch",
    )(*in_hbm(ids, gate_probs.T, tokens, cotangent))
    got = lax.all_to_all(send, ("y", "zl"), split_axis=0, concat_axis=0, tiled=True)
    s = pl.pallas_call(
        compact_kernel,
        out_shape=jax.ShapeDtypeStruct((RECV, w), BF),
        in_specs=[VMEM],
        out_specs=VMEM,
        scratch_shapes=[pltpu.VMEM((8 * CAP, w), F32)],
        compiler_params=limit(4),
        name="compact",
    )(got)

    half = RECV
    z_r = move(s, "zh", 1)
    z_l = move(s, "zh", 3)
    x_r = move(s, "x", 1)
    x_l = move(s, "x", 3)
    x_2 = move(s, "x", 2)
    row_a = jnp.concatenate([s, x_r, x_l, x_2], axis=0)
    near = gate(jnp.concatenate([z_r, z_l], axis=0), x_r, x_l, x_2)
    near_r = move(near, "x", 1)
    near_l = move(near, "x", 3)
    far = move(gate(s, z_r, z_l), "zh", 2)
    row_b = jnp.concatenate([near, near_r, near_l, far], axis=0)
    other_a = move(row_a, "c", 1)
    far_r = move(jnp.concatenate([near_r[:half], gate(far, other_a)], axis=0), "x", 1)
    far_l = move(jnp.concatenate([near_l[half:], far], axis=0), "x", 3)
    far_x = move(gate(x_2, far, near_r, near_l), "zh", 2)
    other_b = move(row_b, "c", 1)
    first = [row_a, other_a, row_b, other_b]

    weights = (gate_w[0], up_w[0], down_w[0])
    size = RECV * 16
    cut = size - row_a.shape[0] * 2 - row_b.shape[0]
    calls = (
        [(q, 0, q.shape[0]) for q in first[:3]] + [(other_b, 0, cut)],
        [(other_b, cut, other_b.shape[0])],
    )
    blk = 1024
    head, tail = calls
    rest = other_b.shape[0] - cut
    meta, part, left = pl.pallas_call(
        functools.partial(first_kernel, [q[1:] for q in head]),
        out_shape=[
            jax.ShapeDtypeStruct((8, size), F32),
            pltpu.HBM((3, hid, d), BF),
            pltpu.HBM((rest, w), BF),
        ],
        in_specs=[VMEM] * (len(head) + 3),
        out_specs=[VMEM, HBM, HBM],
        scratch_shapes=[
            pltpu.VMEM((2, 3, hid, blk), BF),
            pltpu.SemaphoreType.DMA((2, 3)),
            pltpu.SemaphoreType.DMA((1,)),
        ],
        compiler_params=limit(16),
        name="first",
    )(*[q[0] for q in head], *weights)

    row_c = jnp.concatenate([gate(far_r, meta), far_l, far_x], axis=0)
    other_c = move(row_c, "c", 1)
    tail += [(q, 0, q.shape[0]) for q in (row_c, other_c)]
    stored, fact, router = pl.pallas_call(
        functools.partial(last_kernel, [q[1:] for q in tail]),
        out_shape=[
            pltpu.HBM((size - rest, w), BF),
            pltpu.HBM((3, hid, size), BF),
            jax.ShapeDtypeStruct((256, 128), F32),
        ],
        in_specs=[VMEM] * (len(tail) + 4),
        out_specs=[HBM, HBM, VMEM],
        scratch_shapes=[
            pltpu.VMEM((3, hid, size), BF),
            pltpu.SemaphoreType.DMA((len(tail) + 3,)),
        ],
        compiler_params=limit(16),
        name="last",
    )(*[q[0] for q in tail], *weights, meta)
    returned = lax.all_to_all(router, ALL, split_axis=0, concat_axis=0, tiled=True)

    grads = pl.pallas_call(
        backward_kernel,
        out_shape=[jax.ShapeDtypeStruct((1, hid, d), BF)] * 3,
        in_specs=[HBM] * 4,
        out_specs=[HBM] * 3,
        scratch_shapes=[
            pltpu.VMEM((size, w), BF),
            pltpu.VMEM((3, hid, size), BF),
            pltpu.VMEM((3, hid, d), BF),
            pltpu.VMEM((2, 3, hid, blk), BF),
            pltpu.SemaphoreType.DMA((1,)),
            pltpu.SemaphoreType.DMA((d // blk, 4)),
            pltpu.SemaphoreType.DMA((d // blk,)),
            pltpu.SemaphoreType.DMA((2, 3)),
        ],
        compiler_params=limit(32),
        name="backward",
    )(*in_hbm(left, stored, fact, part))

    grad_probs = pl.pallas_call(
        collect_kernel,
        out_shape=jax.ShapeDtypeStruct((2, n), F32),
        in_specs=[VMEM] * 2,
        out_specs=VMEM,
        compiler_params=limit(4),
        name="collect",
    )(returned, ids)
    return (*grads, grad_probs.T)


def solution(mesh):
    fine = Mesh(mesh.devices.reshape([SIZES[a] for a in ALL]), ALL)
    dp, ex = ("x", "zh", "c"), ("y", "zl")
    rows = P(ALL, None)
    kept = P(ex, dp, None)
    return jax.shard_map(
        shards,
        mesh=fine,
        in_specs=(rows,) * 4 + (kept,) * 3,
        out_specs=(kept,) * 3 + (rows,),
        check_vma=False,
    )
```

```python
import functools

import jax
import jax.numpy as jnp
from jax import lax
from jax.experimental import pallas as pl
from jax.experimental.pallas import tpu as pltpu
from jax.sharding import Mesh, PartitionSpec as P

CAP = 4
RECV = 16
BF = jnp.bfloat16
F32 = jnp.float32
I32 = jnp.int32
ALL = ("x", "zh", "c", "y", "zl")
SIZES = {"x": 4, "zh": 4, "c": 2, "y": 4, "zl": 2}
VMEM = pl.BlockSpec(memory_space=pltpu.VMEM)
HBM = pl.BlockSpec(memory_space=pltpu.HBM)


def iota(shape, dim):
    return lax.broadcasted_iota(I32, shape, dim)


def nt(a, b, precision=None):
    return lax.dot_general(
        a, b, (((1,), (1,)), ((), ())), preferred_element_type=F32, precision=precision
    )


def nn(a, b):
    return lax.dot_general(a, b, (((1,), (0,)), ((), ())), preferred_element_type=F32)


def marks(ids):
    n = ids.shape[1]
    rows = iota((8, n), 0)
    first = ids[0:1, :] == rows
    second = ids[1:2, :] == rows
    hit = jnp.where(first | second, 1.0, 0.0).astype(F32)
    earlier = jnp.where(iota((n, n), 0) < iota((n, n), 1), 1.0, 0.0)
    before = nn(hit.astype(BF), earlier.astype(BF))
    return first, second, hit, before


def dispatch_kernel(
    ids_hbm, p_hbm, tok_hbm, cot_hbm, out_ref, ids_ref, p_ref, tok_ref, cot_ref, sems
):
    copies = [
        pltpu.make_async_copy(a, b, sems.at[i])
        for i, (a, b) in enumerate(
            ((ids_hbm, ids_ref), (p_hbm, p_ref), (tok_hbm, tok_ref), (cot_hbm, cot_ref))
        )
    ]
    for c in copies:
        c.start()
    d = tok_ref.shape[1]
    n = tok_ref.shape[0]
    copies[0].wait()
    copies[1].wait()
    me = lax.axis_index(ALL).astype(F32)
    first, _, hit, before = marks(ids_ref[...])
    p = p_ref[...].astype(F32)
    weight = jnp.where(first, p[0:1, :], p[1:2, :])
    spread = jnp.where(iota((8 * CAP, 8), 0) // CAP == iota((8 * CAP, 8), 1), 1.0, 0.0)
    spread = spread.astype(BF)
    hit = nn(spread, hit.astype(BF))
    before = nn(spread, before.astype(BF))
    weight = nn(spread, weight.astype(BF))
    rank = (iota((8 * CAP, n), 0) % CAP).astype(F32)
    pick = jnp.where((hit > 0.5) & (before == rank), 1.0, 0.0)
    one = pick.astype(BF)
    copies[2].wait()
    x = nn(one, tok_ref[...]).astype(BF)
    copies[3].wait()
    dy = nn(one, cot_ref[...]).astype(BF)
    p_col = jnp.sum(pick * weight, axis=1, keepdims=True)
    there = jnp.sum(pick, axis=1, keepdims=True)
    lane = iota((8 * CAP, 128), 1)
    extra = jnp.where(
        lane == 0,
        p_col,
        jnp.where(
            lane == 1, me, jnp.where(lane == 2, rank[:, :128], jnp.where(lane == 3, there, 0.0))
        ),
    ).astype(BF)
    for e in range(8):
        span = slice(e * CAP, (e + 1) * CAP)
        out_ref[e, :, 0:d] = x[span]
        out_ref[e, :, d : 2 * d] = dy[span]
        out_ref[e, :, 2 * d :] = extra[span]


def compact_kernel(in_ref, out_ref, rows_ref):
    w = in_ref.shape[2]
    slots = 8 * CAP
    for e in range(8):
        rows_ref[e * CAP : (e + 1) * CAP, :] = in_ref[e].astype(F32)
    rows = rows_ref[...].astype(BF)
    select = jnp.where(iota((8, 128), 1) == 3, 1.0, 0.0).astype(BF)
    there = nt(select, rows[:, w - 128 :])
    earlier = jnp.where(iota((slots, slots), 0) < iota((slots, slots), 1), 1.0, 0.0).astype(BF)
    place = nn(there.astype(BF), earlier)
    target = iota((RECV, slots), 0).astype(F32)
    pick = jnp.where((there[0:1] > 0.5) & (place[0:1] == target), 1.0, 0.0).astype(BF)
    out_ref[...] = nn(pick, rows).astype(BF)


def forward(pieces, wg_ref, wu_ref, wd_ref):
    d = wg_ref.shape[1]
    x = jnp.concatenate([r[:, 0:d] for r in pieces], axis=0)
    dy = jnp.concatenate([r[:, d : 2 * d] for r in pieces], axis=0)
    extra = jnp.concatenate([r[:, 2 * d :] for r in pieces], axis=0)
    select = jnp.where(iota((8, 128), 0) == iota((8, 128), 1), 1.0, 0.0).astype(BF)
    info = nt(select, extra)
    p = info[0:1]
    gate = nt(wg_ref[...], x)
    up = nt(wu_ref[...], x)
    pulled = nt(wd_ref[...], dy)
    sigma = 1.0 / (1.0 + jnp.exp(-gate))
    silu = gate * sigma
    hidden = silu * up
    router = jnp.sum(hidden.astype(BF).astype(F32) * pulled, axis=0, keepdims=True)
    d_hidden = p * pulled
    dg = (d_hidden * up * sigma * (1.0 + gate * (1.0 - sigma))).astype(BF)
    du = (d_hidden * silu).astype(BF)
    hp = (p * hidden).astype(BF)
    return dg, du, hp, jnp.where(iota(info.shape, 0) == 0, router, info)


def first_kernel(spans, *refs):
    count = len(spans)
    pieces = [r.at[lo:hi] for r, (lo, hi) in zip(refs[:count], spans)]
    wg_ref, wu_ref, wd_ref, meta_ref, part_ref, rows_ref, buf, sems, rows_sem = refs[count:]
    hid, d = wg_ref.shape
    left = pltpu.make_async_copy(
        refs[count - 1].at[spans[-1][1] : refs[count - 1].shape[0]], rows_ref, rows_sem.at[0]
    )
    left.start()
    dg, du, hp, meta_ref[...] = forward(pieces, wg_ref, wu_ref, wd_ref)
    both = jnp.concatenate([dg, du], axis=0)
    blk = buf.shape[3]
    flying = {}
    for j in range(d // blk):
        slot = j % 2
        here = slice(j * blk, (j + 1) * blk)
        there = slice(d + j * blk, d + (j + 1) * blk)
        two = nn(both, jnp.concatenate([r[:, here] for r in pieces], axis=0))
        one = nn(hp, jnp.concatenate([r[:, there] for r in pieces], axis=0))
        for k, value in enumerate((two[:hid], two[hid:], one)):
            if j >= 2:
                flying[k, slot].wait()
            buf[slot, k] = value.astype(BF)
            flying[k, slot] = pltpu.make_async_copy(
                buf.at[slot, k], part_ref.at[k, :, here], sems.at[slot, k]
            )
            flying[k, slot].start()
    left.wait()
    for c in flying.values():
        c.wait()


def last_kernel(spans, *refs):
    count = len(spans)
    pieces = [r.at[lo:hi] for r, (lo, hi) in zip(refs[:count], spans)]
    (
        wg_ref, wu_ref, wd_ref, other_ref, rows_ref, fact_ref, router_ref, fact_buf, sems
    ) = refs[count:]
    copies = []
    at = 0
    for i, (lo, hi) in enumerate(spans):
        if i == 0:
            continue
        n = hi - lo
        copies.append(
            pltpu.make_async_copy(pieces[i], rows_ref.at[at : at + n], sems.at[i])
        )
        copies[-1].start()
        at += n
    *three, meta = forward(pieces, wg_ref, wu_ref, wd_ref)
    for k, value in enumerate(three):
        fact_buf[k] = value
        copies.append(
            pltpu.make_async_copy(fact_buf.at[k], fact_ref.at[k], sems.at[count + k])
        )
        copies[-1].start()
    every = jnp.concatenate([other_ref[...], meta], axis=1)
    n = every.shape[1]
    group = jnp.floor(every[1:2] * 0.125)
    slot = (every[1:2] - 8.0 * group) * CAP + every[2:3]
    own = jnp.where(group == iota((32, n), 0).astype(F32), 1.0, 0.0).astype(BF)
    rest = every[0:1]
    parts = []
    for _ in range(3):
        top = rest.astype(BF)
        parts.append(top.astype(F32))
        rest = rest - parts[-1]
    place = iota((128, n), 0)
    value = jnp.where(place < 32, parts[0], jnp.where(place < 64, parts[1], parts[2]))
    live = ((place % 32).astype(F32) == slot) & (place < 96)
    value = jnp.where(live, value, 0.0).astype(BF)
    moved = nt(own, value)
    mine = (iota((8, 128), 1) % 32) // CAP == iota((8, 128), 0)
    for i in range(32):
        router_ref[8 * i : 8 * i + 8, :] = jnp.where(mine, moved[i : i + 1, :], 0.0)
    for c in copies:
        c.wait()


def backward_kernel(left_hbm, rows_hbm, fact_hbm, part_hbm, *refs):
    outs = refs[:3]
    rows_ref, fact_ref, part_ref, buf, fact_sem, rows_sem, part_sem, out_sem = refs[3:]
    hid, d = part_ref.shape[1:]
    blk = buf.shape[3]
    steps = d // blk
    fact = pltpu.make_async_copy(fact_hbm, fact_ref, fact_sem.at[0])
    fact.start()
    fetch = []
    for j in range(steps):
        some = []
        for k in range(2):
            cols = slice(k * d + j * blk, k * d + (j + 1) * blk)
            cut = left_hbm.shape[0]
            some.append(
                pltpu.make_async_copy(
                    left_hbm.at[:, cols], rows_ref.at[0:cut, cols], rows_sem.at[j, 2 * k]
                )
            )
            some.append(
                pltpu.make_async_copy(
                    rows_hbm.at[:, cols], rows_ref.at[cut:, cols], rows_sem.at[j, 2 * k + 1]
                )
            )
        cols = slice(j * blk, (j + 1) * blk)
        some.append(
            pltpu.make_async_copy(part_hbm.at[:, :, cols], part_ref.at[:, :, cols], part_sem.at[j])
        )
        for c in some:
            c.start()
        fetch.append(some)
    fact.wait()
    both = jnp.concatenate([fact_ref[0], fact_ref[1]], axis=0)
    hp = fact_ref[2]
    flying = {}
    for j in range(steps):
        slot = j % 2
        here = slice(j * blk, (j + 1) * blk)
        there = slice(d + j * blk, d + (j + 1) * blk)
        for c in fetch[j]:
            c.wait()
        two = nn(both, rows_ref[:, here])
        one = nn(hp, rows_ref[:, there])
        for k, value in enumerate((two[:hid], two[hid:], one)):
            if j >= 2:
                flying[k, slot].wait()
            buf[slot, k] = (value + part_ref[k, :, here].astype(F32)).astype(BF)
            flying[k, slot] = pltpu.make_async_copy(
                buf.at[slot, k], outs[k].at[0, :, here], out_sem.at[slot, k]
            )
            flying[k, slot].start()
    for c in flying.values():
        c.wait()


def collect_kernel(got_ref, ids_ref, out_ref):
    first, second, _, before = marks(ids_ref[...])
    total = got_ref[0:8, :]
    for i in range(1, got_ref.shape[0] // 8):
        total = total + got_ref[8 * i : 8 * i + 8, :]
    value = jnp.zeros(before.shape, F32)
    for j in range(CAP):
        mine = iota(total.shape, 1) % CAP == j
        sums = jnp.sum(jnp.where(mine, total, 0.0), axis=1, keepdims=True)
        value = value + jnp.where(before == j, sums, 0.0)
    out_ref[0:1, :] = jnp.sum(jnp.where(first, value, 0.0), axis=0, keepdims=True)
    out_ref[1:2, :] = jnp.sum(jnp.where(second, value, 0.0), axis=0, keepdims=True)


def in_hbm(*arrays):
    return [pltpu.with_memory_space_constraint(a, pltpu.HBM) for a in arrays]


def limit(mib):
    return pltpu.CompilerParams(vmem_limit_bytes=mib * 1024 * 1024)


def move(a, axis, shift):
    n = SIZES[axis]
    return lax.ppermute(a, axis, [(i, (i + shift) % n) for i in range(n)])


def gate(a, *after):
    return lax.optimization_barrier((a,) + after)[0]


def shards(tokens, cotangent, expert_ids, gate_probs, gate_w, up_w, down_w):
    n, d = tokens.shape
    hid = gate_w.shape[1]
    w = 2 * d + 128
    ids = expert_ids.T
    send = pl.pallas_call(
        dispatch_kernel,
        out_shape=jax.ShapeDtypeStruct((8, CAP, w), BF),
        in_specs=[HBM] * 4,
        out_specs=VMEM,
        scratch_shapes=[
            pltpu.VMEM((2, n), I32),
            pltpu.VMEM((2, n), BF),
            pltpu.VMEM((n, d), BF),
            pltpu.VMEM((n, d), BF),
            pltpu.SemaphoreType.DMA((4,)),
        ],
        compiler_params=limit(8),
        name="dispatch",
    )(*in_hbm(ids, gate_probs.T, tokens, cotangent))
    got = lax.all_to_all(send, ("y", "zl"), split_axis=0, concat_axis=0, tiled=True)
    s = pl.pallas_call(
        compact_kernel,
        out_shape=jax.ShapeDtypeStruct((RECV, w), BF),
        in_specs=[VMEM],
        out_specs=VMEM,
        scratch_shapes=[pltpu.VMEM((8 * CAP, w), F32)],
        compiler_params=limit(4),
        name="compact",
    )(got)

    half = RECV
    z_r = move(s, "zh", 1)
    z_l = move(s, "zh", 3)
    x_r = move(s, "x", 1)
    x_l = move(s, "x", 3)
    x_2 = move(s, "x", 2)
    row_a = jnp.concatenate([s, x_r, x_l, x_2], axis=0)
    near = gate(jnp.concatenate([z_r, z_l], axis=0), x_r, x_l, x_2)
    near_r = move(near, "x", 1)
    near_l = move(near, "x", 3)
    far = move(gate(s, z_r, z_l), "zh", 2)
    row_b = jnp.concatenate([near, near_r, near_l, far], axis=0)
    other_a = move(row_a, "c", 1)
    far_r = move(jnp.concatenate([near_r[:half], gate(far, other_a)], axis=0), "x", 1)
    far_l = move(jnp.concatenate([near_l[half:], far], axis=0), "x", 3)
    far_x = move(gate(x_2, far, near_r, near_l), "zh", 2)
    other_b = move(row_b, "c", 1)
    first = [row_a, other_a, row_b, other_b]

    weights = (gate_w[0], up_w[0], down_w[0])
    size = RECV * 16
    cut = size - row_a.shape[0] * 2 - row_b.shape[0]
    calls = (
        [(q, 0, q.shape[0]) for q in first[:3]] + [(other_b, 0, cut)],
        [(other_b, cut, other_b.shape[0])],
    )
    blk = 1024
    head, tail = calls
    rest = other_b.shape[0] - cut
    meta, part, left = pl.pallas_call(
        functools.partial(first_kernel, [q[1:] for q in head]),
        out_shape=[
            jax.ShapeDtypeStruct((8, size), F32),
            pltpu.HBM((3, hid, d), BF),
            pltpu.HBM((rest, w), BF),
        ],
        in_specs=[VMEM] * (len(head) + 3),
        out_specs=[VMEM, HBM, HBM],
        scratch_shapes=[
            pltpu.VMEM((2, 3, hid, blk), BF),
            pltpu.SemaphoreType.DMA((2, 3)),
            pltpu.SemaphoreType.DMA((1,)),
        ],
        compiler_params=limit(16),
        name="first",
    )(*[q[0] for q in head], *weights)

    row_c = gate(far_r, meta)
    other_c = move(row_c, "c", 1)
    row_d = jnp.concatenate([far_l, far_x], axis=0)
    other_d = move(row_d, "c", 1)
    tail += [(q, 0, q.shape[0]) for q in (row_c, other_c, row_d, other_d)]
    stored, fact, router = pl.pallas_call(
        functools.partial(last_kernel, [q[1:] for q in tail]),
        out_shape=[
            pltpu.HBM((size - rest, w), BF),
            pltpu.HBM((3, hid, size), BF),
            jax.ShapeDtypeStruct((256, 128), F32),
        ],
        in_specs=[VMEM] * (len(tail) + 4),
        out_specs=[HBM, HBM, VMEM],
        scratch_shapes=[
            pltpu.VMEM((3, hid, size), BF),
            pltpu.SemaphoreType.DMA((len(tail) + 3,)),
        ],
        compiler_params=limit(16),
        name="last",
    )(*[q[0] for q in tail], *weights, meta)
    returned = lax.all_to_all(router, ALL, split_axis=0, concat_axis=0, tiled=True)

    grads = pl.pallas_call(
        backward_kernel,
        out_shape=[jax.ShapeDtypeStruct((1, hid, d), BF)] * 3,
        in_specs=[HBM] * 4,
        out_specs=[HBM] * 3,
        scratch_shapes=[
            pltpu.VMEM((size, w), BF),
            pltpu.VMEM((3, hid, size), BF),
            pltpu.VMEM((3, hid, d), BF),
            pltpu.VMEM((2, 3, hid, blk), BF),
            pltpu.SemaphoreType.DMA((1,)),
            pltpu.SemaphoreType.DMA((d // blk, 4)),
            pltpu.SemaphoreType.DMA((d // blk,)),
            pltpu.SemaphoreType.DMA((2, 3)),
        ],
        compiler_params=limit(32),
        name="backward",
    )(*in_hbm(left, stored, fact, part))

    grad_probs = pl.pallas_call(
        collect_kernel,
        out_shape=jax.ShapeDtypeStruct((2, n), F32),
        in_specs=[VMEM] * 2,
        out_specs=VMEM,
        compiler_params=limit(4),
        name="collect",
    )(returned, ids)
    return (*grads, grad_probs.T)


def solution(mesh):
    fine = Mesh(mesh.devices.reshape([SIZES[a] for a in ALL]), ALL)
    dp, ex = ("x", "zh", "c"), ("y", "zl")
    rows = P(ALL, None)
    kept = P(ex, dp, None)
    return jax.shard_map(
        shards,
        mesh=fine,
        in_specs=(rows,) * 4 + (kept,) * 3,
        out_specs=(kept,) * 3 + (rows,),
        check_vma=False,
    )
```
